32 devices in a mesh: dp: 8 (over z, y), tensor: 4 (over x, core).
Axes of the slice: x: 2, y: 2, z: 4, core: 2. Of those that a mesh axis runs over, the one named last changes fastest.
Arguments:
- tokens: bfloat16 [3152, 768], P('dp'), may hold values from -6 to 6
- norm_params: float32 [4, 768], replicated, may hold values from 0.5 to 1.5
- w_qkv: bfloat16 [3, 768, 768], P(None, None, 'tensor'), may hold values from -0.21875 to 0.21875
- b_qv: float32 [2, 768], P(None, 'tensor'), may hold values from -3 to 3
- w_out: bfloat16 [768, 768], P('tensor'), may hold values from -1.75 to 1.75
- b_out: float32 [768], replicated, may hold values from -3 to 3
- w_router: bfloat16 [768, 4], replicated, may hold values from -0.4375 to 0.4375
- w_in: bfloat16 [4, 768, 3072], P(None, None, 'tensor'), may hold values from -0.21875 to 0.21875
- b_in: float32 [4, 3072], P(None, 'tensor'), may hold values from -3 to 3
- w_back: bfloat16 [4, 3072, 768], P(None, 'tensor'), may hold values from -0.3125 to 0.3125
- b_back: float32 [4, 768], replicated, may hold values from -3 to 3
- routes: int32 [3152, 2], P('dp'), may hold values from 0 to 3, all different within a row; in each aligned block of 394 rows (0 to 393, 394 to 787, ...) at most 263 rows name the same one
- img_count: int32 [8], P('dp'), may hold values from 1 to 2, as said below
- cotangent: bfloat16 [3152, 768], P('dp'), may hold values from -6 to 6
Outputs:
- out_act: bfloat16 [3152, 768], P('dp')
- in_grad: float32 [3152, 768], P('dp')
- g_norms: float32 [4, 768], replicated
- g_qkv: float32 [3, 768, 768], P(None, 'dp', 'tensor')
- g_qv: float32 [2, 768], P(None, 'tensor')
- g_out: float32 [768, 768], P('tensor', 'dp')
- g_bout: float32 [768], replicated
- g_router: float32 [768, 4], replicated
- g_in: float32 [4, 768, 3072], P(None, 'dp', 'tensor')
- g_bin: float32 [4, 3072], P(None, 'tensor')
- g_back: float32 [4, 3072, 768], P(None, 'tensor', 'dp')
- g_bback: float32 [4, 768], replicated
The draws below stay inside these ranges and needn't reach their ends.
Inputs may be any that keep to these rules, and one draw needn't show every extreme that they name: In the rows of one group of devices along dp no expert is named by more than 263 routes; the two experts of a token differ. The first img_count[g] image slots of group g hold live images, the rest are empty.
All inputs are finite; a program needn't handle non-finite values.
Results may differ from the reference program's by a relative error of at most 0.028.
The reference program's roundings to bfloat16 on the way count: a program that leaves them out, or rounds other values in their place, can miss the bound.
Values sent between devices are 32-bit elements; how exact they have to be, the bound alone decides.
No kernel may reach another device: no remote copies, remote signals or barrier semaphores. Data moves between devices by JAX's collectives and lax.ppermute only.
A program may use at most 128 MiB of HBM per device.

```python
import math
import jax
import jax.numpy as jnp
import numpy as np
from jax import lax

D = 768
HEADS = 12
HD = 64
FF = 3072
SEQ = 197
E = 4
IMG_DEV = 2
TOK_DEV = 394
CAP = 263
GROUPS = 8
TOKENS = 3152


def draw_img_count(key, part):
    draw_one, draw_two, draw_three = jax.random.split(key, 3)
    counts = jax.random.randint(draw_one, (GROUPS,), IMG_DEV - 1, IMG_DEV + 1)
    top_at = jax.random.randint(draw_two, (), 0, GROUPS)
    bottom_at = (top_at + 1 + jax.random.randint(draw_three, (), 0, GROUPS - 1)) % GROUPS
    return counts.at[top_at].set(IMG_DEV).at[bottom_at].set(IMG_DEV - 1).astype(jnp.int32)


def spiked(values, own_key, source, target, blocks, factor):
    owner, partner = [(jnp.arange(values.shape[dim]) // (values.shape[dim] // blocks)).reshape([-1 if axis == dim else 1 for axis in range(values.ndim)]) for dim in (source, target)]
    chosen = jax.random.permutation(own_key, blocks)[partner]
    strong = (owner == chosen) | (owner == (partner + blocks // 2) % blocks)
    return jnp.where(strong, factor * values, values)


def shard_levels(rng, extent, shards, smallest, top_value):
    loudness, own = 1.0, jax.random.fold_in(rng, 6)
    for axis_at, parts in shards:
        draws = jnp.exp(jax.random.uniform(jax.random.fold_in(own, axis_at), (parts,), jnp.float32, smallest / len(shards), top_value / len(shards)))
        loudness = loudness * jnp.repeat(draws, extent[axis_at] // parts).reshape([-1 if axis == axis_at else 1 for axis in range(len(extent))])
    return loudness


def deal_out(rng, own, number, rows, number_of, top, most, skew):
    ranking = jax.random.permutation(rng, number_of)
    packed, ordinary = load_shares(number_of, rows * top, most, skew, True), load_shares(number_of, rows * top, most, skew, False)
    places = jnp.arange(number_of)

    def named(lengths, offset_by):
        used = int((lengths > 0).sum())
        fixed = max(1, used // 4)
        passed = fixed + (places - fixed + offset_by * (used - fixed)) % max(1, number_of - fixed)
        return jnp.zeros((number_of,), jnp.int32).at[ranking[jnp.where(places < fixed, places, passed)]].set(jnp.asarray(lengths, jnp.int32))

    lengths = jnp.where(number % 4 == 0, named(packed, number // 4), named(ordinary, number - number // 4 - 1))
    mixed = jax.random.permutation(jax.random.fold_in(own, 3), number_of)
    giver, taker = mixed[0:number_of // 2 * 2:2], mixed[1:number_of // 2 * 2:2]
    margin = jnp.minimum(lengths[giver] - 1, most - lengths[taker]) // 2
    margin = jnp.where((giver == ranking[0]) | (taker == ranking[0]) | (lengths[taker] == 0), 0, jnp.maximum(margin, 0))
    passed = jax.random.randint(jax.random.fold_in(own, 4), (number_of // 2,), 0, 1 << 20) % (margin + 1)
    lengths = lengths.at[giver].add(-passed).at[taker].add(passed)
    labels = jnp.searchsorted(jnp.cumsum(lengths), jnp.arange(rows * top), side="right").astype(jnp.int32)
    table = labels.reshape(top, rows).T
    table = table[jax.random.permutation(jax.random.fold_in(own, 1), rows)]
    offset_by = jax.random.randint(jax.random.fold_in(own, 2), (rows, 1), 0, top)
    return jnp.take_along_axis(table, (jnp.arange(top)[None, :] + offset_by) % top, axis=1)


def load_shares(amount, total, most, lean, full):
    loads = [(1 << 20) // math.isqrt(standing ** lean) + 1 for standing in range(1, amount + 1)]
    largest = most if full else min(most, max(-(-total // amount), total * loads[0] // sum(loads)))
    least = 1 if total - largest >= amount - 1 else 0
    given, rest = [largest] + [least] * (amount - 1), total - largest - least * (amount - 1)
    while rest > 0:
        candidates = [i for i in range(1, amount) if given[i] < largest] or [i for i in range(1, amount) if given[i] < most]
        pool, budget = sum([loads[i] for i in candidates]), rest
        for i in candidates:
            more = min(most - given[i], max(1, budget * loads[i] // pool), rest)
            given[i] = given[i] + more
            rest = rest - more
    return np.array(given)


def scatter_about(own_key, shape, deviation, most, shards=(), held_as=jnp.bfloat16):
    drawn = jax.random.normal(own_key, shape, jnp.float32) * deviation
    if len(shards) > 0:
        drawn = shard_levels(own_key, shape, shards, -0.22, 0.18) * drawn
    return jnp.clip(drawn, min=-most, max=most).astype(held_as)


def heavy_noise(stream_key, extent, width, most, cuts, heavy, kind=jnp.bfloat16):
    drawn = width * jax.random.normal(stream_key, extent, jnp.float32)
    if cuts:
        drawn = drawn * shard_levels(stream_key, extent, cuts, -0.22, 0.18)
    return jnp.clip(spiked(drawn, jax.random.fold_in(stream_key, 3), *heavy), -most, most).astype(kind)


def setup_inputs(seed: int = 0) -> dict:
    streams_of = jax.random.split(jax.random.key(seed), 15)
    tokens = heavy_noise(streams_of[0], (TOKENS, D), 1.0, 6.0, ((0, 8),), (0, 1, 8, 2.0))
    norm_params = jnp.clip(jax.random.uniform(streams_of[1], (4, D), jnp.float32, 0.5, 1.5), 0.5, 1.5)
    w_qkv = scatter_about(streams_of[2], (3, D, D), D ** -0.5, 0.21875, ((2, 4),))
    b_qv = scatter_about(streams_of[3], (2, D), 0.5, 3.0, ((1, 4),), jnp.float32)
    w_out = scatter_about(streams_of[4], (D, D), (D // 64) ** -0.5, 1.75, ((0, 4),))
    b_out = scatter_about(streams_of[5], (D,), 0.5, 3.0, (), jnp.float32)
    w_router = scatter_about(streams_of[6], (D, E), (D // 4) ** -0.5, 0.4375)
    w_in = scatter_about(streams_of[7], (E, D, FF), D ** -0.5, 0.21875, ((2, 4),))
    b_in = scatter_about(streams_of[8], (E, FF), 0.5, 3.0, ((1, 4),), jnp.float32)
    w_back = scatter_about(streams_of[9], (E, FF, D), (FF // 8) ** -0.5, 0.3125, ((1, 4),))
    b_back = scatter_about(streams_of[10], (E, D), 0.5, 3.0, (), jnp.float32)
    routes_keys = jax.random.split(jax.random.fold_in(streams_of[11], 1), TOKENS // TOK_DEV)
    routes_turns = jax.random.permutation(jax.random.fold_in(streams_of[11], 3), TOKENS // TOK_DEV)
    routes = jax.vmap(lambda own, number: deal_out(jax.random.fold_in(streams_of[11], 2), own, number, TOK_DEV, E, 2, CAP, 2))(routes_keys, routes_turns).reshape((TOKENS, 2))
    img_count = draw_img_count(jax.random.fold_in(streams_of[14], 71), 0)
    cotangent = heavy_noise(streams_of[13], (TOKENS, D), 1.0, 6.0, ((0, 8),), (0, 1, 8, 2.0))
    return {"tokens": tokens, "norm_params": norm_params, "w_qkv": w_qkv, "b_qv": b_qv, "w_out": w_out, "b_out": b_out, "w_router": w_router, "w_in": w_in, "b_in": b_in, "w_back": w_back, "b_back": b_back, "routes": routes, "img_count": img_count, "cotangent": cotangent}


EPS = 1e-06
HIGH = lax.Precision.HIGHEST

@jax.custom_vjp
def low(v):
    return lax.optimization_barrier(v.astype(jnp.bfloat16)).astype(jnp.float32)

@jax.custom_vjp
def low_back(v):
    return v

def low_keep(v):
    return (low(v), None)

def low_pass(kept, grad):
    return (grad,)

def back_keep(v):
    return (v, None)

def back_low(kept, grad):
    return (low(grad),)
low.defvjp(low_keep, low_pass)
low_back.defvjp(back_keep, back_low)

def both_ways(value):
    return low(low_back(value))

def layer_norm(value, gain, shift):
    mean_v = lax.optimization_barrier(jnp.mean(value, -1, keepdims=True))
    centred = value - mean_v
    var_v = lax.optimization_barrier(jnp.mean(centred * centred, -1, keepdims=True))
    return centred * lax.rsqrt(var_v + EPS) * gain + shift

def reference(tokens, norm_params, w_qkv, b_qv, w_out, b_out, w_router, w_in, b_in, w_back, b_back, routes, img_count, cotangent):
    tok_total = tokens.shape[0]
    images = tok_total // SEQ
    row_ids = jnp.arange(tok_total, dtype=jnp.int32)
    group_of = row_ids // (IMG_DEV * SEQ)
    slot_of = row_ids % (IMG_DEV * SEQ) // SEQ
    live = (slot_of < img_count[group_of]).astype(jnp.float32)[:, None]
    expert_ids = jnp.arange(E, dtype=jnp.int32)
    chosen = lax.optimization_barrier(jnp.sum((routes[:, :, None] == expert_ids[None, None, :]).astype(jnp.float32), 1))
    scale = HD ** (-0.5)

    def attend(triple):
        q_img, k_img, v_img = triple
        scores = low_back(scale * jnp.einsum('qhd,khd->hqk', q_img, k_img, precision=HIGH))
        probs = low(jax.nn.softmax(scores, axis=-1))
        return both_ways(jnp.einsum('hqk,khd->qhd', probs, v_img, precision=HIGH))

    def per_image(value):
        return value.reshape(images, SEQ, HEADS, HD)

    def forward(params):
        x_in, norm_p, qkv_w, qv_b, out_w, out_b, router_w, in_w, in_b, back_w, back_b = params
        n_one = low(layer_norm(x_in, norm_p[0], norm_p[1]))
        q_all = both_ways(jnp.dot(n_one, qkv_w[0], precision=HIGH) + qv_b[0])
        k_all = both_ways(jnp.dot(n_one, qkv_w[1], precision=HIGH))
        v_all = both_ways(jnp.dot(n_one, qkv_w[2], precision=HIGH) + qv_b[1])
        context = lax.map(jax.checkpoint(attend), (per_image(q_all), per_image(k_all), per_image(v_all)))
        context = context.reshape(tok_total, HEADS * HD)
        hidden = x_in + low_back(jnp.dot(context, out_w, precision=HIGH)) + out_b
        n_two = low(layer_norm(hidden, norm_p[2], norm_p[3]))
        gates = jax.nn.softmax(low_back(jnp.dot(n_two, router_w, precision=HIGH)), axis=-1)
        weights_re = gates * chosen

        def expert_step(total, expert_args):
            e_in, e_bin, e_back, e_idx = expert_args
            pre = low_back(jnp.dot(n_two, e_in, precision=HIGH) + e_bin)
            act = low(jax.nn.gelu(pre, approximate=False))
            branch = low_back(jnp.dot(act, e_back, precision=HIGH))
            column = lax.optimization_barrier(jnp.sum(weights_re * (expert_ids == e_idx).astype(jnp.float32), -1, keepdims=True))
            return (total + column * branch, None)
        moe, _ = lax.scan(jax.checkpoint(expert_step), jnp.zeros_like(x_in), (in_w, in_b, back_w, expert_ids))
        moe = moe + jnp.dot(weights_re, back_b, precision=HIGH)
        return (hidden + moe) * live
    params = tuple((item.astype(jnp.float32) for item in (tokens, norm_params, w_qkv, b_qv, w_out, b_out, w_router, w_in, b_in, w_back, b_back)))
    result, pullback = jax.vjp(forward, params)
    grads = pullback(cotangent.astype(jnp.float32))[0]
    return (result.astype(jnp.bfloat16), grads[0], grads[1], grads[2], grads[3], grads[4], grads[5], grads[6], grads[7], grads[8], grads[9], grads[10])
```

```python
import jax
import jax.numpy as jnp
from jax import lax
from jax.experimental import pallas as pl
from jax.experimental.pallas import tpu as pltpu
from jax.sharding import PartitionSpec as P

HD = 64
SEQ = 197
CAP = 263


EPS = 1e-06


def normalize(value, gain, shift):
    mean_v = jnp.mean(value, -1, keepdims=True)
    centred = value - mean_v
    inv_std = lax.rsqrt(jnp.mean(centred * centred, -1, keepdims=True) + EPS)
    normed = centred * inv_std
    return (normed * gain + shift, normed, inv_std)


def norm_back(grad, normed, inv_std, gain):
    scaled = grad * gain
    inner = jnp.mean(scaled * normed, -1, keepdims=True)
    return (scaled - jnp.mean(scaled, -1, keepdims=True) - normed * inner) * inv_std


def gelu_exact(value):
    return jax.nn.gelu(value, approximate=False)


def body_any(
    tokens,
    norm_params,
    w_qkv,
    b_qv,
    w_out,
    b_out,
    w_router,
    w_in,
    b_in,
    w_back,
    b_back,
    routes,
    img_count,
    cotangent,
):
    row_count, width = tokens.shape
    images = row_count // SEQ
    heads_loc = w_qkv.shape[2] // HD
    experts = w_in.shape[0]
    scale = HD ** (-0.5)
    x_full = tokens.astype(jnp.float32)
    slot_of = jnp.arange(row_count, dtype=jnp.int32) // SEQ
    live = (slot_of < img_count[0]).astype(jnp.float32)[:, None]
    grad_y = cotangent.astype(jnp.float32) * live
    norm_one, normed_one, inv_one = normalize(x_full, norm_params[0], norm_params[1])
    act_one = norm_one.astype(jnp.bfloat16)
    project = jnp.einsum("rd,jdc->jrc", act_one, w_qkv, preferred_element_type=jnp.float32)
    q_loc = (project[0] + b_qv[0]).astype(jnp.bfloat16).reshape(images, SEQ, heads_loc, HD)
    k_loc = project[1].astype(jnp.bfloat16).reshape(images, SEQ, heads_loc, HD)
    v_loc = (project[2] + b_qv[1]).astype(jnp.bfloat16).reshape(images, SEQ, heads_loc, HD)
    scores = scale * jnp.einsum("iqhd,ikhd->ihqk", q_loc, k_loc, preferred_element_type=jnp.float32)
    log_total = jax.nn.logsumexp(scores, axis=-1, keepdims=True)
    probs_low = jnp.exp(scores - log_total).astype(jnp.bfloat16)
    context = jnp.einsum("ihqk,ikhd->iqhd", probs_low, v_loc, preferred_element_type=jnp.float32)
    context = context.astype(jnp.bfloat16).reshape(row_count, heads_loc * HD)
    attn = lax.psum(jnp.dot(context, w_out, preferred_element_type=jnp.float32), "tensor")
    hidden = x_full + attn + b_out
    norm_two, normed_two, inv_two = normalize(hidden, norm_params[2], norm_params[3])
    act_two = norm_two.astype(jnp.bfloat16)
    logits = jnp.dot(act_two, w_router, preferred_element_type=jnp.float32)
    gates = jax.nn.softmax(logits, axis=-1)
    pick_int = (routes[:, :, None] == jnp.arange(experts, dtype=jnp.int32)[None, None, :]).astype(
        jnp.int32
    )
    picks = pick_int.astype(jnp.float32)
    gate_k = jnp.sum(picks * gates[:, None, :], -1)
    flat_pick = pick_int.reshape(row_count * 2, experts)
    position = jnp.sum((jnp.cumsum(flat_pick, 0) - flat_pick) * flat_pick, -1)
    slot_id = routes.reshape(-1) * CAP + position
    token_of = (
        jnp.full((experts * CAP,), row_count, jnp.int32)
        .at[slot_id]
        .set(jnp.arange(row_count * 2, dtype=jnp.int32) // 2)
    )
    padded = jnp.concatenate([act_two, jnp.zeros((1, width), jnp.bfloat16)], 0)
    dispatched = padded[token_of].reshape(experts, CAP, width)
    pre_act = (
        jnp.einsum("ecd,edf->ecf", dispatched, w_in, preferred_element_type=jnp.float32)
        + b_in[:, None, :]
    )
    hidden_low = gelu_exact(pre_act).astype(jnp.bfloat16)
    expert_out = jnp.einsum(
        "ecf,efd->ecd", hidden_low, w_back, preferred_element_type=jnp.float32
    ).reshape(experts * CAP, width)
    route_out = expert_out[slot_id].reshape(row_count, 2, width)
    moe_part = jnp.sum(gate_k[:, :, None] * route_out, 1)
    dots_part = jnp.sum(route_out * grad_y[:, None, :], -1)
    moe, dots = lax.psum((moe_part, dots_part), "tensor")
    bias_route = jnp.einsum("rke,ed->rkd", picks, b_back)
    moe_total = moe + jnp.sum(gate_k[:, :, None] * bias_route, 1)
    out_act = ((hidden + moe_total) * live).astype(jnp.bfloat16)
    dgate = dots + jnp.sum(bias_route * grad_y[:, None, :], -1)
    g_bback = jnp.einsum("rke,rd->ed", picks * gate_k[:, :, None], grad_y)
    du_route = (
        (gate_k[:, :, None] * grad_y[:, None, :]).astype(jnp.bfloat16).reshape(row_count * 2, width)
    )
    du_slots = (
        jnp.zeros((experts * CAP, width), jnp.bfloat16)
        .at[slot_id]
        .set(du_route)
        .reshape(experts, CAP, width)
    )
    g_back = jnp.einsum("ecf,ecd->efd", hidden_low, du_slots, preferred_element_type=jnp.float32)
    dhidden = jnp.einsum("ecd,efd->ecf", du_slots, w_back, preferred_element_type=jnp.float32)
    _, gelu_pull = jax.vjp(gelu_exact, pre_act)
    dpre = gelu_pull(dhidden)[0].astype(jnp.bfloat16)
    g_bin = jnp.sum(dpre.astype(jnp.float32), 1)
    g_in = jnp.einsum("ecd,ecf->edf", dispatched, dpre, preferred_element_type=jnp.float32)
    dslots = jnp.einsum("ecf,edf->ecd", dpre, w_in, preferred_element_type=jnp.float32).reshape(
        experts * CAP, width
    )
    da2_part = jnp.sum(dslots[slot_id].reshape(row_count, 2, width), 1)
    dgates = jnp.einsum("rk,rke->re", dgate, picks)
    dlogits = gates * (dgates - jnp.sum(gates * dgates, -1, keepdims=True))
    dlog_low = dlogits.astype(jnp.bfloat16)
    g_router = jnp.einsum("rd,re->de", act_two, dlog_low, preferred_element_type=jnp.float32)
    router_back = jnp.einsum("re,de->rd", dlog_low, w_router, preferred_element_type=jnp.float32)
    da_two = lax.psum(da2_part, "tensor") + router_back
    g_gain_two = jnp.sum(da_two * normed_two, 0)
    g_shift_two = jnp.sum(da_two, 0)
    dhid = grad_y + norm_back(da_two, normed_two, inv_two, norm_params[2])
    g_bout = jnp.sum(dhid, 0)
    dhid_low = dhid.astype(jnp.bfloat16)
    g_out = jnp.einsum("rc,rd->cd", context, dhid_low, preferred_element_type=jnp.float32)
    dcontext = jnp.einsum("rd,cd->rc", dhid_low, w_out, preferred_element_type=jnp.float32)
    dcontext = dcontext.astype(jnp.bfloat16).reshape(images, SEQ, heads_loc, HD)
    again = scale * jnp.einsum("iqhd,ikhd->ihqk", q_loc, k_loc, preferred_element_type=jnp.float32)
    probs = jnp.exp(again - log_total)
    dprobs = jnp.einsum("iqhd,ikhd->ihqk", dcontext, v_loc, preferred_element_type=jnp.float32)
    dv_loc = jnp.einsum(
        "ihqk,iqhd->ikhd", probs.astype(jnp.bfloat16), dcontext, preferred_element_type=jnp.float32
    ).astype(jnp.bfloat16)
    dscore = (probs * (dprobs - jnp.sum(probs * dprobs, -1, keepdims=True))).astype(jnp.bfloat16)
    dq_loc = (
        scale * jnp.einsum("ihqk,ikhd->iqhd", dscore, k_loc, preferred_element_type=jnp.float32)
    ).astype(jnp.bfloat16)
    dk_loc = (
        scale * jnp.einsum("ihqk,iqhd->ikhd", dscore, q_loc, preferred_element_type=jnp.float32)
    ).astype(jnp.bfloat16)
    dstack = jnp.stack([dq_loc, dk_loc, dv_loc], 0).reshape(3, row_count, heads_loc * HD)
    g_qkv = jnp.einsum("rd,jrc->jdc", act_one, dstack, preferred_element_type=jnp.float32)
    g_qv = jnp.stack(
        [jnp.sum(dstack[0].astype(jnp.float32), 0), jnp.sum(dstack[2].astype(jnp.float32), 0)], 0
    )
    da1_part = jnp.einsum("jrc,jdc->rd", dstack, w_qkv, preferred_element_type=jnp.float32)
    da_one = lax.psum(da1_part, "tensor")
    g_gain_one = jnp.sum(da_one * normed_one, 0)
    g_shift_one = jnp.sum(da_one, 0)
    in_grad = dhid + norm_back(da_one, normed_one, inv_one, norm_params[0])
    g_norms = jnp.stack([g_gain_one, g_shift_one, g_gain_two, g_shift_two], 0)
    g_qkv_s, g_out_s, g_in_s, g_back_s = (
        lax.psum_scatter(g_qkv, "dp", scatter_dimension=1, tiled=True),
        lax.psum_scatter(g_out, "dp", scatter_dimension=1, tiled=True),
        lax.psum_scatter(g_in, "dp", scatter_dimension=1, tiled=True),
        lax.psum_scatter(g_back, "dp", scatter_dimension=2, tiled=True),
    )
    g_norms_s, g_qv_s, g_bout_s, g_router_s, g_bin_s, g_bback_s = lax.psum(
        (g_norms, g_qv, g_bout, g_router, g_bin, g_bback), "dp"
    )
    return (
        out_act,
        in_grad,
        g_norms_s,
        g_qkv_s,
        g_qv_s,
        g_out_s,
        g_bout_s,
        g_router_s,
        g_in_s,
        g_bin_s,
        g_back_s,
        g_bback_s,
    )


PAD = 208


def send(value, axis, flip):
    size = 8 if axis == "dp" else 4
    return lax.ppermute(value, axis, [(i, i ^ flip) for i in range(size)])


def pick(flag, one, two):
    return jnp.where(flag == 0, one, two)


def in_order(flag, mine, theirs, dim):
    return pick(
        flag, jnp.concatenate([mine, theirs], dim), jnp.concatenate([theirs, mine], dim)
    )


def mm(left, right):
    return jnp.dot(left, right, preferred_element_type=jnp.float32)


def mm_nt(left, right):
    return lax.dot_general(left, right, (((1,), (1,)), ((), ())), preferred_element_type=jnp.float32)


def pad_rows(value, images):
    width = value.shape[-1]
    return jnp.pad(value.reshape(images, SEQ, width), ((0, 0), (0, PAD - SEQ), (0, 0))).reshape(
        images * PAD, width
    )


def cut_rows(value, images):
    width = value.shape[-1]
    return value.reshape(images, PAD, width)[:, :SEQ].reshape(images * SEQ, width)


def block_of(value, index, size, dim):
    return lax.dynamic_slice_in_dim(value, index * size, size, dim)


ROOT_HALF = 0.7071067811865476
ROOT_TWO_PI = 0.3989422804014327


def expert_kernel(
    at_ref, act_ref, dy_ref, weight_ref, w_in_ref, b_in_ref, w_back_ref, keep0_ref, send0_ref,
    low_ref, dpre_ref, dots_ref, keep_ref, send_ref, bias_ref
):
    expert, core = at_ref[0], at_ref[1]
    half = keep_ref.shape[1]
    pre = jnp.dot(act_ref[...], w_in_ref[0], preferred_element_type=jnp.float32) + b_in_ref[0]
    back = mm_nt(dy_ref[...], w_back_ref[0])
    cdf = 0.5 + 0.5 * lax.erf(pre * ROOT_HALF)
    low = (pre * cdf).astype(jnp.bfloat16)
    low_ref[...] = low
    lanes = jnp.zeros((low.shape[0], 128), jnp.float32)
    for at in range(0, low.shape[1], 128):
        lanes += low[:, at : at + 128].astype(jnp.float32) * back[:, at : at + 128]
    dots_ref[0] = jnp.sum(lanes.T, 0, keepdims=True)
    lane = lax.broadcasted_iota(jnp.int32, weight_ref.shape, 1)
    weight = jnp.sum(jnp.where(lane == expert, weight_ref[...], 0.0), -1, keepdims=True)
    slope = cdf + pre * (ROOT_TWO_PI * jnp.exp(-0.5 * pre * pre))
    dpre = (back * weight * slope).astype(jnp.bfloat16)
    dpre_ref[...] = dpre

    @pl.when(pl.program_id(0) == 0)
    def _():
        bias_ref[...] = jnp.zeros_like(bias_ref)

    bias_ref[...] += jnp.sum(dpre.astype(jnp.float32), 0, keepdims=True)
    keep_at = pl.multiple_of(core * half, 128)
    send_at = pl.multiple_of((1 - core) * half, 128)
    keep_ref[...] = keep0_ref[...] + mm_nt(dpre, w_in_ref[0, pl.ds(keep_at, half), :])
    send_ref[...] = send0_ref[...] + mm_nt(dpre, w_in_ref[0, pl.ds(send_at, half), :])


def expert_pass(where, act, dy_low, weights, w_in, b_in, w_back, keep0, send0, tile):
    rows, width = act.shape
    hidden = w_in.shape[2]
    half = width // 2
    row = lambda n: pl.BlockSpec((tile, n), lambda i, at: (i, 0))
    one = lambda a, b: pl.BlockSpec((1, a, b), lambda i, at: (at[0], 0, 0))
    return pl.pallas_call(
        expert_kernel,
        out_shape=(
            jax.ShapeDtypeStruct((rows, hidden), jnp.bfloat16),
            jax.ShapeDtypeStruct((rows, hidden), jnp.bfloat16),
            jax.ShapeDtypeStruct((rows // tile, 1, tile), jnp.float32),
            jax.ShapeDtypeStruct((rows, half), jnp.float32),
            jax.ShapeDtypeStruct((rows, half), jnp.float32),
            jax.ShapeDtypeStruct((1, hidden), jnp.float32),
        ),
        grid_spec=pltpu.PrefetchScalarGridSpec(
            num_scalar_prefetch=1,
            grid=(rows // tile,),
            in_specs=[
                row(width),
                row(width),
                row(weights.shape[1]),
                one(width, hidden),
                one(1, hidden),
                one(hidden, width),
                row(half),
                row(half),
            ],
            out_specs=(
                row(hidden),
                row(hidden),
                pl.BlockSpec((1, 1, tile), lambda i, at: (i, 0, 0)),
                row(half),
                row(half),
                pl.BlockSpec((1, hidden), lambda i, at: (0, 0)),
            ),
        ),
        compiler_params=pltpu.CompilerParams(vmem_limit_bytes=48 * 2**20),
        name="expert_pass",
    )(where, act, dy_low, weights, w_in, b_in, w_back, keep0, send0)


def after(value, *others):
    return lax.optimization_barrier((value, *others))[0]


def body_block(
    tokens,
    norm_params,
    w_qkv,
    b_qv,
    w_out,
    b_out,
    w_router,
    w_in,
    b_in,
    w_back,
    b_back,
    routes,
    img_count,
    cotangent,
):
    row_count, width = tokens.shape
    images = row_count // SEQ
    rows = images * PAD
    cols = w_qkv.shape[2]
    heads_loc = cols // HD
    experts = w_in.shape[0]
    mine = experts // 2
    half = width // 2
    part = width // 8
    scale = HD ** (-0.5)
    core = lax.axis_index("tensor") % 2
    group = lax.axis_index("dp")
    y_at = group % 2
    z_low = (group // 2) % 2
    z_high = group // 4

    slot_of = jnp.arange(rows, dtype=jnp.int32)
    inside = slot_of % PAD < SEQ
    live = ((slot_of // PAD < img_count[0]) & inside).astype(jnp.float32)[:, None]
    x_full = pad_rows(tokens, images).astype(jnp.float32)
    dy = pad_rows(cotangent, images).astype(jnp.float32) * live
    picks = jnp.sum(
        (routes[:, :, None] == jnp.arange(experts, dtype=jnp.int32)[None, None, :]).astype(
            jnp.float32
        ),
        1,
    )
    chosen = pad_rows(picks, images)

    def to_partner(block):
        got = send(block, "dp", 2)
        return in_order(core, got, send(got, "tensor", 1), 1)

    with_live = send(jnp.concatenate([chosen, live], 1).T, "dp", 2).T
    chosen_there = with_live[:, :experts]
    dy_there = to_partner(block_of(dy, core, half, 1)) * with_live[:, experts:]
    w_back_two = block_of(w_back, z_low, mine, 0)

    norm_one, normed_one, inv_one = normalize(x_full, norm_params[0], norm_params[1])
    act_one = norm_one.astype(jnp.bfloat16)
    project = jnp.einsum("rd,jdc->jrc", act_one, w_qkv, preferred_element_type=jnp.float32)
    q_loc = (project[0] + b_qv[0]).astype(jnp.bfloat16).reshape(images, PAD, heads_loc, HD)
    k_loc = project[1].astype(jnp.bfloat16).reshape(images, PAD, heads_loc, HD)
    v_loc = (project[2] + b_qv[1]).astype(jnp.bfloat16).reshape(images, PAD, heads_loc, HD)
    scores = scale * jnp.einsum("iqhd,ikhd->ihqk", q_loc, k_loc, preferred_element_type=jnp.float32)
    key_ok = (jnp.arange(PAD) < SEQ)[None, None, None, :]
    scores = jnp.where(key_ok, scores, -jnp.inf)
    log_total = jax.nn.logsumexp(scores, axis=-1, keepdims=True)
    probs = jnp.exp(scores - log_total)
    probs_low = probs.astype(jnp.bfloat16)
    context = jnp.einsum("ihqk,ikhd->iqhd", probs_low, v_loc, preferred_element_type=jnp.float32)
    context = context.astype(jnp.bfloat16).reshape(rows, cols)

    def sum_over_tensor(make):
        got = send(make(1 - core), "tensor", 1)
        total = make(core) + got
        return total + send(total, "tensor", 2)

    attn_half = sum_over_tensor(lambda at: mm(context, block_of(w_out, at, half, 1)))
    hid_half = (
        block_of(x_full, core, half, 1) + attn_half + lax.dynamic_slice_in_dim(b_out, core * half, half)
    )
    hidden = in_order(core, hid_half, send(hid_half, "tensor", 1), 1)
    hid_there = to_partner(hid_half)

    def route(value, pick_re):
        normed, hat, inv = normalize(value, norm_params[2], norm_params[3])
        low = normed.astype(jnp.bfloat16)
        gates = jax.nn.softmax(mm(low, w_router), axis=-1)
        return low, hat, inv, gates, gates * pick_re

    act_two, normed_two, inv_two, gates, weights = route(hidden, chosen)
    act_there, _, _, _, weights_there = route(hid_there, chosen_there)
    act_all = jnp.concatenate([act_two, act_there], 0)
    weights_all = jnp.concatenate([weights, weights_there], 0)
    dy_all = jnp.concatenate([dy, dy_there], 0)
    dy_low = dy_all.astype(jnp.bfloat16)
    weights_two = block_of(weights_all, z_low, mine, 1)

    act_t = act_all.T.reshape(4, 2, part, 2 * rows)
    dy_t = dy_low.T.reshape(4, 2, part, 2 * rows)
    def two_rows(left, at, count):
        return lax.dynamic_index_in_dim(left, at, 1, keepdims=False).reshape(4 * part, count)

    def first_send(left, right):
        out = mm(two_rows(left, 1 - y_at, right.shape[0]), right).reshape(4, part, -1)
        return out, send(out, "dp", 1)

    def first_sum(left, right, got):
        total = mm(two_rows(left, y_at, right.shape[0]), right).reshape(4, part, -1) + got
        return block_of(total, z_high, 2, 0), block_of(total, 1 - z_high, 2, 0)

    def split_low(pair):
        return (
            lax.dynamic_index_in_dim(pair, z_low, 0, keepdims=False),
            lax.dynamic_index_in_dim(pair, 1 - z_low, 0, keepdims=False),
        )

    def du_of(e):
        return (
            dy_t.astype(jnp.float32) * weights_two[:, e][None, None, None, :]
        ).astype(jnp.bfloat16)

    hid_low, dpre, dots, g_bin_two = [], [], [], []
    du_t = [du_of(e) for e in range(mine)]
    sent, got_one = [], []
    keep = away = jnp.zeros((2 * rows, half), jnp.float32)
    act_in = act_all
    for e in range(mine):
        where = jnp.stack([z_low * mine + e, core]).astype(jnp.int32)
        low, dp, dot, keep, away, bias = expert_pass(
            where, act_in, dy_low, weights_all, w_in, b_in[:, None, :], w_back, keep, away, PAD
        )
        hid_low.append(low)
        dpre.append(dp)
        dots.append(dot.reshape(2 * rows))
        g_bin_two.append(bias[0])
        out, got = first_send(du_t[e], low)
        sent.append(out)
        got_one.append(got)
        act_in = after(act_in, out)

    def home(keep, away):
        total = keep + send(away, "tensor", 1)
        total = total[:rows] + send(total[rows:], "dp", 2)
        return total + send(total, "tensor", 2)

    total = keep + send(away, "tensor", 1)
    total = after(total, sent[1])
    got_total = send(total[rows:], "dp", 2)
    mid = [first_sum(du_t[0], after(hid_low[0], total), got_one[0])]
    got_mid = [send(mid[0][1], "dp", 4)]

    def next_chunk(right):
        out, got = first_send(act_t, right)
        sent.append(out)
        got_one.append(got)

    def serve(left, right, at):
        mid.append(first_sum(left, right, got_one[at]))
        got_mid.append(send(mid[at][1], "dp", 4))

    next_chunk(after(dpre[0], mid[0][1]))
    total = after(total[:rows], mid[0][1], sent[2]) + got_total
    got_total = send(total, "tensor", 2)
    serve(du_t[1], after(hid_low[1], total), 1)
    next_chunk(after(dpre[1], mid[1][1]))
    hid_late = [after(low, total) for low in hid_low]
    da2_half = after(total, mid[1][1], sent[3]) + got_total
    da2_main = in_order(core, da2_half, send(da2_half, "tensor", 1), 1)
    dots = jnp.stack(dots, 0)
    dots = dots + send(dots, "tensor", 1)
    dots = dots + send(dots, "tensor", 2)
    dots = in_order(z_low, dots[:, :rows], send(dots[:, rows:], "dp", 2), 0)

    dgates = (
        dots.T + lax.dot_general(dy, b_back, (((1,), (1,)), ((), ())), precision=lax.Precision.HIGHEST)
    ) * chosen
    dlogits = gates * (dgates - jnp.sum(gates * dgates, -1, keepdims=True))
    dlog_low = dlogits.astype(jnp.bfloat16)
    da_two = da2_main + mm_nt(dlog_low, w_router)
    dhid = dy + norm_back(da_two, normed_two, inv_two, norm_params[2])
    dhid_low = dhid.astype(jnp.bfloat16)

    def moe_columns(at):
        total = jnp.zeros((2 * rows, half), jnp.float32)
        for e in range(mine):
            total = total + weights_two[:, e : e + 1] * mm(hid_late[e], block_of(w_back_two[e], at, half, 1))
        return total

    moe_half = home(moe_columns(core), moe_columns(1 - core))
    moe = in_order(core, moe_half, send(moe_half, "tensor", 1), 1)
    for e in range(experts):
        moe = moe + weights[:, e : e + 1] * b_back[e]
    out_act = cut_rows(((hidden + moe) * live).astype(jnp.bfloat16), images)

    dcontext = mm_nt(dhid_low, w_out).astype(jnp.bfloat16).reshape(images, PAD, heads_loc, HD)
    dprobs = jnp.einsum("iqhd,ikhd->ihqk", dcontext, v_loc, preferred_element_type=jnp.float32)
    dv_loc = jnp.einsum(
        "ihqk,iqhd->ikhd", probs_low, dcontext, preferred_element_type=jnp.float32
    ).astype(jnp.bfloat16)
    dscore = (probs * (dprobs - jnp.sum(probs * dprobs, -1, keepdims=True))).astype(jnp.bfloat16)
    serve(act_t, after(dpre[0], dscore), 2)
    dscore = after(dscore, mid[2][1])
    dq_loc = (
        scale * jnp.einsum("ihqk,ikhd->iqhd", dscore, k_loc, preferred_element_type=jnp.float32)
    ).astype(jnp.bfloat16)
    dk_loc = (
        scale * jnp.einsum("ihqk,iqhd->ikhd", dscore, q_loc, preferred_element_type=jnp.float32)
    ).astype(jnp.bfloat16)
    dcat = jnp.concatenate([d.reshape(rows, cols) for d in (dq_loc, dk_loc, dv_loc)], 1)

    def da1_columns(at):
        w_at = block_of(w_qkv, at, half, 1)
        return mm_nt(dcat, jnp.concatenate([w_at[0], w_at[1], w_at[2]], 1))

    da1_send = da1_columns(1 - core)
    da1_got = send(da1_send, "tensor", 1)
    act_one_t = act_one.T.reshape(4, 2, part, rows)
    q_sent, q_got = first_send(act_one_t, after(dcat, da1_send))
    da1_keep = da1_columns(core)
    norm_sums = []
    for at_half in (0, 1):
        piece = pick(core, da1_keep, da1_send) if at_half == 0 else pick(core, da1_send, da1_keep)
        hat = normed_one[:, at_half * half : (at_half + 1) * half]
        norm_sums.append(jnp.stack([jnp.sum(piece * hat, 0), jnp.sum(piece, 0)], 0))
    norm_sums = jnp.concatenate(norm_sums, 1)
    norm_sums = norm_sums + send(norm_sums, "tensor", 1)
    da1_half = da1_keep + da1_got
    da1_there = send(da1_half, "tensor", 2)
    norm_sums = after(norm_sums, da1_half)
    norm_sums = norm_sums + send(norm_sums, "tensor", 2)
    serve(act_t, after(dpre[1], da1_half), 3)
    da1_half = after(da1_half, mid[3][1]) + da1_there
    da_one = in_order(core, da1_half, send(da1_half, "tensor", 1), 1)
    in_grad = dhid + norm_back(da_one, normed_one, inv_one, norm_params[0])
    in_grad = cut_rows(in_grad, images)
    dhid_t = dhid_low.T.reshape(4, 2, part, rows)
    o_sent, o_got = first_send(dhid_t, context)
    q_mid = first_sum(act_one_t, after(dcat, mid[3][1]), q_got)
    q_pair = q_mid[0] + send(q_mid[1], "dp", 4)
    q_keep, q_away = split_low(q_pair)
    g_qkv = (q_keep + send(q_away, "dp", 2)).reshape(part, 3, cols).swapaxes(0, 1)
    o_mid = first_sum(dhid_t, context, o_got)
    o_keep, o_away = split_low(o_mid[0] + send(o_mid[1], "dp", 4))
    g_out = (o_keep + send(o_away, "dp", 2)).T

    final = []
    for pair, got in zip(mid, got_mid):
        ours, theirs = split_low(pair[0] + got)
        final.append((ours, send(theirs, "dp", 2)))

    def assemble(pairs):
        ours = jnp.stack([p[0] for p in pairs], 0)
        theirs = jnp.stack([p[1] for p in pairs], 0)
        return in_order(z_low, ours, theirs, 0)

    g_back = jnp.swapaxes(assemble(final[:mine]), 1, 2)
    g_in = assemble(final[mine:])

    def all_groups(pack):
        for flip in (1, 2, 4):
            pack = pack + send(pack, "dp", flip)
        return pack

    g_router = mm(dlog_low.T, act_two)
    g_bin_two = jnp.stack(g_bin_two, 0)
    g_bin = in_order(z_low, g_bin_two, jnp.zeros_like(g_bin_two), 0)
    g_bback = lax.dot_general(
        weights, dy, (((0,), (0,)), ((), ())), precision=lax.Precision.HIGHEST
    )
    dsum = jnp.sum(dcat.astype(jnp.float32), 0)
    pack = all_groups(
        jnp.concatenate(
            [
                norm_sums,
                jnp.sum(da_two * normed_two, 0)[None],
                jnp.sum(da_two, 0)[None],
                jnp.sum(dhid, 0)[None],
                g_router,
                g_bback,
                g_bin,
                jnp.pad(dsum, (0, width - 3 * cols))[None],
            ],
            0,
        )
    )
    g_qv = jnp.stack([pack[-1, :cols], pack[-1, 2 * cols : 3 * cols]], 0)
    return (
        out_act,
        in_grad,
        pack[:4],
        g_qkv,
        g_qv,
        g_out,
        pack[4],
        pack[5 : 5 + experts].T,
        g_in,
        pack[5 + 2 * experts : 5 + 3 * experts],
        g_back,
        pack[5 + experts : 5 + 2 * experts],
    )


def solution(mesh):
    placed = (
        P("dp", None),
        P(),
        P(None, None, "tensor"),
        P(None, "tensor"),
        P("tensor", None),
        P(),
        P(),
        P(None, None, "tensor"),
        P(None, "tensor"),
        P(None, "tensor", None),
        P(),
        P("dp", None),
        P("dp"),
        P("dp", None),
    )
    sizes = dict(mesh.shape)
    body = body_block if (sizes["dp"], sizes["tensor"]) == (8, 4) else body_any
    return jax.shard_map(
        body,
        mesh=mesh,
        in_specs=placed,
        out_specs=(
            P("dp", None),
            P("dp", None),
            P(),
            P(None, "dp", "tensor"),
            P(None, "tensor"),
            P("tensor", "dp"),
            P(),
            P(),
            P(None, "dp", "tensor"),
            P(None, "tensor"),
            P(None, "tensor", "dp"),
            P(),
        ),
        check_vma=False,
    )
```
